256 devices in a mesh: tm: 32 (over z, y_lo, core), gz: 8 (over y_hi, x).
Axes of the slice: x: 4, y: 4 (y_hi: 2, y_lo: 2; y = y_hi * 2 + y_lo), z: 8, core: 2. Of those that a mesh axis runs over, the one named last changes fastest.
Arguments:
- states: float32 [32, 4, 32, 128, 128], P('tm', None, 'gz'), may hold values from -6 to 6
- first_unconverged: int32 [1], replicated, may hold values from 0 to 31
- window_offset: int32 [1], replicated, may hold values from 0 to 63
- summaries: float32 [64], replicated, may hold values from -5 to 5
- cond_weight: float32 [64, 32], replicated, may hold values from -0.75 to 0.75
- time_gain: float32 [32], replicated, may hold values from -4 to 4
- conv_weight: float32 [27, 32, 4], replicated, may hold values from -0.625 to 0.625
- out_weight: float32 [4, 32], replicated, may hold values from -1 to 1
Outputs:
- new_states: float32 [32, 4, 32, 128, 128], P('tm', None, 'gz')
The draws below stay inside these ranges and needn't reach their ends.
All inputs are finite; a program needn't handle non-finite values.
Results may differ from the reference program's by a relative error of at most 0.0001.
Values sent between devices are 32-bit elements; how exact they have to be, the bound alone decides.
A program may use at most 128 MiB of HBM per device.

```python
import jax
import jax.numpy as jnp
from jax import lax

CH = 4
HID = 32
NSUM = 64
NY = 128
NX = 128
STEPS = 32
NZ = 32


def block_levels(key, extent, cuts, least, top_value):
    level = 1.0
    for dim, blocks in cuts:
        draws = jax.random.uniform(jax.random.fold_in(jax.random.fold_in(key, 6), dim), (blocks,), jnp.float32, least / len(cuts), top_value / len(cuts))
        level = level * jnp.repeat(jnp.exp(draws), extent[dim] // blocks).reshape((-1,) + (1,) * (len(extent) - 1 - dim))
    return level


def bell_draw(own_key, extent, scale, most, cuts=(), kind=jnp.bfloat16):
    array = scale * jax.random.normal(own_key, extent, jnp.float32)
    if cuts:
        array = array * block_levels(own_key, extent, cuts, -0.22, 0.18)
    return jnp.clip(array, -most, most).astype(kind)


def setup_inputs(seed: int = 0) -> dict:
    key_list = jax.random.split(jax.random.key(seed), 9)
    return {
        "states": bell_draw(key_list[0], (STEPS, CH, NZ, NY, NX), 1.0, 6.0, ((0, 32), (2, 8)), jnp.float32),
        "first_unconverged": jax.random.randint(key_list[1], (1,), 0, STEPS).astype(jnp.int32),
        "window_offset": jax.random.randint(key_list[2], (1,), 0, 64).astype(jnp.int32),
        "summaries": bell_draw(key_list[3], (NSUM,), 1.0, 5.0, (), jnp.float32),
        "cond_weight": bell_draw(key_list[4], (NSUM, HID), NSUM ** -0.5, 0.75, (), jnp.float32),
        "time_gain": bell_draw(key_list[5], (HID,), 1.0, 4.0, (), jnp.float32),
        "conv_weight": bell_draw(key_list[6], (27, HID, CH), (27 * CH) ** -0.5, 0.625, (), jnp.float32),
        "out_weight": bell_draw(key_list[7], (CH, HID), HID ** -0.5, 1.0, (), jnp.float32),
    }


STEP_SIZE = 0.125


def drift_field(field, step_time, condition, time_gain, conv_weight, out_weight):
    hidden = jnp.zeros((conv_weight.shape[1],) + field.shape[1:], jnp.float32)
    for shift_z in (-1, 0, 1):
        for shift_y in (-1, 0, 1):
            for shift_x in (-1, 0, 1):
                offset = 9 * (shift_z + 1) + 3 * (shift_y + 1) + (shift_x + 1)
                shifted = jnp.roll(field, (-shift_z, -shift_y, -shift_x), axis=(1, 2, 3))
                hidden = hidden + jnp.einsum("ci,izyx->czyx", conv_weight[offset], shifted, precision=lax.Precision.HIGHEST)
    hidden = hidden + (condition + step_time * time_gain)[:, None, None, None]
    activation = jax.nn.silu(hidden)
    return STEP_SIZE * jnp.einsum("ic,czyx->izyx", out_weight, activation, precision=lax.Precision.HIGHEST)


def reference(states, first_unconverged, window_offset, summaries, cond_weight, time_gain, conv_weight, out_weight):
    condition = jnp.dot(summaries, cond_weight, precision=lax.Precision.HIGHEST, preferred_element_type=jnp.float32)
    step_index = jnp.arange(STEPS, dtype=jnp.int32)
    step_times = 1.0 - (window_offset[0] + step_index).astype(jnp.float32) / float(STEPS + 64)

    def one_step(pair_item):
        return drift_field(pair_item[0], pair_item[1], condition, time_gain, conv_weight, out_weight)

    increments = lax.map(one_step, (states, step_times))
    running = jnp.cumsum(increments, axis=0)
    earlier = jnp.concatenate([jnp.zeros_like(running[:1]), running[:-1]], axis=0)
    anchor = lax.dynamic_index_in_dim(states, first_unconverged[0].astype(jnp.int32), 0, keepdims=False)
    return anchor[None] + earlier
```

```python
import functools

import jax
import jax.numpy as jnp
import numpy as np
from jax import lax
from jax.experimental import pallas as pl
from jax.experimental.pallas import tpu as pltpu
from jax.sharding import PartitionSpec as P

STEP_SIZE = 0.125
MESH = pl.DeviceIdType.MESH

BLOCK = 80
WINDOW = 3 * BLOCK
TILE = 8
PIECES = 4
EARLY = 4
F32, BF16 = jnp.float32, jnp.bfloat16


def selector(channels, planes):
    chosen = np.zeros((27, channels, planes, WINDOW), np.float32)
    for b in range(3):
        for e in range(3):
            for zo in range(planes):
                for a in range(3):
                    zi = zo + a - 1
                    for i in range(channels):
                        if zi < 0:
                            plane = channels * planes + i
                        elif zi >= planes:
                            plane = channels * planes + channels + i
                        else:
                            plane = i * planes + zi
                        chosen[9 * a + 3 * b + e, i, zo, BLOCK * b + 24 * e + plane] = 1.0
    return chosen


def split(value):
    high = value.astype(BF16)
    return high, (value - high.astype(F32)).astype(BF16)


def kernel(
    first_ref, state_hbm, weight_ref, mix_ref, out_ref,
    st, halo, patch_hi, patch_lo, weight_hl, mix_hl, inc,
    mine, pm, dr, ds, pv, ur, us, yr, ys, fs,
    local_sem, halo_send, halo_recv, pm_send, pm_recv, d_send, d_recv,
    e_send, e_recv, u_send, u_recv, y_send, y_recv, f_send, f_recv,
):
    planes16 = st.shape[0]
    channels, planes = state_hbm.shape[0], state_hbm.shape[1]
    half = st.shape[2]
    rows = 2 * half
    chunks = half // TILE
    t, g = lax.axis_index("tm"), lax.axis_index("gz")
    count = lax.axis_size("tm")
    levels = count // 4
    ring = lax.axis_size("gz")
    core = t % 2
    other = 1 - core
    side = (t // 2) % 2
    z = t // 4
    top = levels - 1
    partner = t + 1 - 2 * core
    across = t + 2 - 4 * side
    after, before = (g + 1) % ring, (g + ring - 1) % ring

    fetch = pltpu.make_async_copy(state_hbm, st.reshape(channels, planes, 2, half, 128), local_sem)
    fetch.start()

    barrier = pltpu.get_barrier_semaphore()
    pl.semaphore_signal(barrier, inc=1, device_id={"tm": partner}, device_id_type=MESH)
    pl.semaphore_signal(barrier, inc=1, device_id={"tm": across}, device_id_type=MESH)
    pl.semaphore_signal(barrier, inc=1, device_id={"gz": after}, device_id_type=MESH)
    pl.semaphore_signal(barrier, inc=1, device_id={"gz": before}, device_id_type=MESH)

    pl.semaphore_signal(barrier, inc=1, device_id={"tm": (t + 4) % count}, device_id_type=MESH)
    pl.semaphore_signal(barrier, inc=1, device_id={"tm": (t + count - 4) % count}, device_id_type=MESH)
    pl.semaphore_wait(barrier, 6)

    span = half // PIECES

    def halo_copies(piece):
        at = pl.ds(span * piece, span)
        up = pltpu.make_async_remote_copy(
            src_ref=state_hbm.at[:, planes - 1, :, at, :],
            dst_ref=halo.at[0:channels, :, at, :],
            send_sem=halo_send.at[0, piece], recv_sem=halo_recv.at[0, piece],
            device_id={"gz": after}, device_id_type=MESH,
        )
        down = pltpu.make_async_remote_copy(
            src_ref=state_hbm.at[:, 0, :, at, :],
            dst_ref=halo.at[channels : 2 * channels, :, at, :],
            send_sem=halo_send.at[1, piece], recv_sem=halo_recv.at[1, piece],
            device_id={"gz": before}, device_id_type=MESH,
        )
        return up, down

    halos = {}
    for piece in [PIECES - 1] + list(range(PIECES - 1)):
        halos[piece] = halo_copies(piece)
        for copy in halos[piece]:
            copy.start()

    fetch.wait()

    is_first = jnp.where(first_ref[0] == t, 1.0, 0.0).astype(F32)

    @pl.loop(0, planes16)
    def _(p):
        mine[p] = st[p] * is_first

    pm_copy = pltpu.make_async_remote_copy(
        src_ref=mine.at[:, other], dst_ref=pm, send_sem=pm_send, recv_sem=pm_recv,
        device_id={"tm": partner}, device_id_type=MESH,
    )
    pm_copy.start()

    high, low = split(weight_ref[...])
    wide = high.shape[0]
    weight_hl[0:wide] = high
    weight_hl[wide : 2 * wide] = low
    high, low = split(mix_ref[...])
    weight16 = high.shape[0]
    mix_hl[0:weight16] = high
    mix_hl[weight16 : 2 * weight16] = low

    st2 = st.reshape(planes16 * rows, 128)
    halo2 = halo.reshape(2 * channels * rows, 128)
    inc2 = inc.reshape(planes16 * rows, 128)
    ones = jnp.ones((8, 128), F32)

    def build(y):
        where = pl.multiple_of(BLOCK * (y + 1), 16)
        for lane, row in ((0, (y + rows) % rows), (128, (y + half) % rows)):
            body = jnp.concatenate(
                [st2[pl.ds(row, planes16, stride=rows), :], halo2[pl.ds(row, 2 * channels, stride=rows), :]], axis=0
            )
            full = jnp.concatenate([pltpu.roll(body, 1, 1), body, pltpu.roll(body, 127, 1), ones], axis=0)
            high, low = split(full)
            patch_hi[pl.ds(where, BLOCK), lane : lane + 128] = high
            patch_lo[pl.ds(where, BLOCK), lane : lane + 128] = low

    def drift(y):
        window = pl.ds(pl.multiple_of(BLOCK * y, 16), WINDOW)
        both = jnp.dot(weight_hl[...], patch_hi[window, :], preferred_element_type=F32)
        hidden = both[0:wide] + both[wide : 2 * wide] + jnp.dot(
            weight_hl[0:wide], patch_lo[window, :], preferred_element_type=F32
        )
        active = hidden + hidden * jnp.tanh(hidden)
        high, low = split(active)
        both = jnp.dot(mix_hl[...], high, preferred_element_type=F32)
        result = both[0:weight16] + both[weight16 : 2 * weight16] + jnp.dot(
            mix_hl[0:weight16], low, preferred_element_type=F32
        )
        inc2[pl.ds(y, planes16, stride=rows), :] = result[:, 0:128]
        inc2[pl.ds(y + half, planes16, stride=rows), :] = result[:, 128:256]

    def to(refs, j, sends, recvs, device):
        src, dst = refs
        return pltpu.make_async_remote_copy(
            src_ref=src, dst_ref=dst, send_sem=sends.at[j], recv_sem=recvs.at[j],
            device_id={"tm": device}, device_id_type=MESH,
        )

    def at(j):
        return pl.ds(pl.multiple_of(TILE * j, TILE), TILE)

    def e_copy(j):
        return to((inc.at[:, other, at(j), :], pv.at[:, at(j), :]), j, e_send, e_recv, partner)

    def d_copy(j):
        return to((ds.at[:, at(j), :], dr.at[:, at(j), :]), j, d_send, d_recv, t - 4)

    def u_copy(j):
        return to((us.at[:, at(j), :], ur.at[:, at(j), :]), j, u_send, u_recv, t + 4)

    def y_copy(j):
        return to((ys.at[:, at(j), :], yr.at[:, at(j), :]), j, y_send, y_recv, across)

    def f_copy(j):
        return to((fs.at[:, at(j), :], out_ref.at[:, core, at(j), :]), j, f_send, f_recv, partner)

    pm_copy.wait()

    d_slot = 2 * (top - z)
    u_slot = 2 * z + 1 + EARLY
    y_slot = jnp.maximum(u_slot, d_slot + 1)
    f_slot = y_slot + 2
    need = {0: [PIECES - 1, 0]}
    for piece in range(1, PIECES):
        if piece < PIECES - 1:
            need[span * piece // TILE - 1] = [piece]

    def turn(n, _):
        k = n - EARLY
        for chunk, pieces in need.items():
            @pl.when(k == chunk)
            def _():
                for piece in pieces:
                    for copy in halos[piece]:
                        copy.wait_recv()

        @pl.when(k == 0)
        def _():
            build(-1)
            build(0)

        @pl.when((k >= 0) & (k < chunks))
        def _():
            first = TILE * k

            @pl.loop(0, TILE // 2)
            def _(n):
                build(first + 2 * n + 1)
                build(first + 2 * n + 2)

            @pl.loop(0, TILE // 2)
            def _(n):
                drift(first + 2 * n)
                drift(first + 2 * n + 1)

            e_copy(k).start()

        jd = n - d_slot

        @pl.when((jd >= 0) & (jd < chunks))
        def _():
            rows_j = at(jd)

            @pl.when(z < top)
            def _():
                d_copy(jd).wait_recv()

            @pl.when(z == top)
            def _():
                dr[:, rows_j, :] = jnp.zeros((planes16, TILE, 128), F32)

            @pl.when(z > 0)
            def _():
                ds[:, rows_j, :] = dr[:, rows_j, :] + mine[:, core, rows_j, :] + pm[:, rows_j, :]
                d_copy(jd).start()

        ju = n - u_slot

        @pl.when((ju >= 0) & (ju < chunks))
        def _():
            rows_j = at(ju)
            e_copy(ju).wait_recv()

            @pl.when(z > 0)
            def _():
                u_copy(ju).wait_recv()

            @pl.when(z == 0)
            def _():
                ur[:, rows_j, :] = jnp.zeros((planes16, TILE, 128), F32)

            @pl.when(z < top)
            def _():
                us[:, rows_j, :] = (
                    ur[:, rows_j, :] + inc[:, core, rows_j, :] + pv[:, rows_j, :]
                    + mine[:, core, rows_j, :] + pm[:, rows_j, :]
                )
                u_copy(ju).start()

        jy = n - y_slot

        @pl.when((jy >= 0) & (jy < chunks))
        def _():
            rows_j = at(jy)
            total = ur[:, rows_j, :] + dr[:, rows_j, :] + mine[:, core, rows_j, :] + pm[:, rows_j, :]
            own = inc[:, core, rows_j, :] + pv[:, rows_j, :]
            ys[:, rows_j, :] = jnp.where(side == 0, total + own, total)
            y_copy(jy).start()

        jf = n - f_slot

        @pl.when((jf >= 0) & (jf < chunks))
        def _():
            rows_j = at(jf)
            y_copy(jf).wait_recv()
            total = (
                ur[:, rows_j, :] + dr[:, rows_j, :] + mine[:, core, rows_j, :] + pm[:, rows_j, :] + yr[:, rows_j, :]
            )
            out_ref[:, core, rows_j, :] = jnp.where(core == 1, total + pv[:, rows_j, :], total)
            fs[:, rows_j, :] = jnp.where(core == 0, total + inc[:, core, rows_j, :], total)
            f_copy(jf).start()

        return 0

    lax.fori_loop(0, chunks + 2 * top + 3 + EARLY, turn, 0)

    for pair in halos.values():
        for copy in pair:
            copy.wait_send()

    @pl.loop(0, chunks)
    def _(j):
        e_copy(j).wait_send()
        y_copy(j).wait_send()
        f_copy(j).wait()

        @pl.when(z > 0)
        def _():
            d_copy(j).wait_send()

        @pl.when(z < top)
        def _():
            u_copy(j).wait_send()


def shards(
    states, first_unconverged, window_offset, summaries, cond_weight, time_gain, conv_weight, out_weight
):
    channels, planes, rows, cols = states.shape[1:]
    hidden = conv_weight.shape[1]
    half = rows // 2
    steps = states.shape[0] * lax.axis_size("tm")
    step = lax.axis_index("tm")
    step_time = 1.0 - (window_offset[0] + step).astype(F32) / float(steps + 64)
    condition = jnp.dot(summaries, cond_weight, precision=lax.Precision.HIGHEST, preferred_element_type=F32)
    offset = condition + step_time * time_gain
    chosen = selector(channels, planes)
    weight = jnp.einsum("oci,oizk->zck", conv_weight, chosen, precision=lax.Precision.HIGHEST)
    marker = np.zeros((WINDOW,), np.float32)
    marker[72] = 1.0
    weight = 0.5 * (weight + offset[None, :, None] * marker).reshape(planes * hidden, WINDOW)
    mix = STEP_SIZE * jnp.einsum("ic,zw->izwc", out_weight, np.eye(planes, dtype=np.float32), precision=lax.Precision.HIGHEST)
    mix = mix.reshape(channels * planes, planes * hidden)
    state = states.reshape(channels, planes, 2, half, cols)
    p16 = channels * planes
    chunks = half // TILE
    half_shape = pltpu.VMEM((p16, half, cols), F32)
    whole_shape = pltpu.VMEM((p16, 2, half, cols), F32)
    dma = pltpu.SemaphoreType.DMA
    out = pl.pallas_call(
        kernel,
        name="picard",
        out_shape=jax.ShapeDtypeStruct((p16, 2, half, cols), F32),
        in_specs=[
            pl.BlockSpec(memory_space=pltpu.SMEM),
            pl.BlockSpec(memory_space=pl.ANY),
            pl.BlockSpec(memory_space=pltpu.VMEM),
            pl.BlockSpec(memory_space=pltpu.VMEM),
        ],
        out_specs=pl.BlockSpec(memory_space=pltpu.VMEM),
        scratch_shapes=[
            whole_shape,
            pltpu.VMEM((2 * channels, 2, half, cols), F32),
            pltpu.VMEM(((half + 2) * BLOCK, 256), BF16),
            pltpu.VMEM(((half + 2) * BLOCK, 256), BF16),
            pltpu.VMEM((2 * planes * hidden, WINDOW), BF16),
            pltpu.VMEM((2 * p16, planes * hidden), BF16),
            whole_shape,
            whole_shape,
        ]
        + [half_shape] * 9
        + [dma, dma((2, PIECES)), dma((2, PIECES)), dma, dma]
        + [dma((chunks,))] * 10,
        compiler_params=pltpu.CompilerParams(
            collective_id=0, has_side_effects=True, vmem_limit_bytes=48 * 1024 * 1024
        ),
    )(first_unconverged, state, weight, mix)
    return out.reshape(states.shape)


def solution(mesh):
    placed = (P("tm", None, "gz", None, None), P(), P(), P(), P(), P(), P(), P())
    return jax.shard_map(
        shards,
        mesh=mesh,
        in_specs=placed,
        out_specs=P("tm", None, "gz", None, None),
        check_vma=False,
    )
```

```python
import functools

import jax
import jax.numpy as jnp
import numpy as np
from jax import lax
from jax.experimental import pallas as pl
from jax.experimental.pallas import tpu as pltpu
from jax.sharding import PartitionSpec as P

STEP_SIZE = 0.125
MESH = pl.DeviceIdType.MESH

BLOCK = 80
WINDOW = 3 * BLOCK
TILE = 8
PIECES = 4
EARLY = 4
PARTS = 2
F32, BF16 = jnp.float32, jnp.bfloat16


def selector(channels, planes):
    chosen = np.zeros((27, channels, planes, WINDOW), np.float32)
    for b in range(3):
        for e in range(3):
            for zo in range(planes):
                for a in range(3):
                    zi = zo + a - 1
                    for i in range(channels):
                        if zi < 0:
                            plane = channels * planes + i
                        elif zi >= planes:
                            plane = channels * planes + channels + i
                        else:
                            plane = i * planes + zi
                        chosen[9 * a + 3 * b + e, i, zo, BLOCK * b + 24 * e + plane] = 1.0
    return chosen


def split(value):
    high = value.astype(BF16)
    return high, (value - high.astype(F32)).astype(BF16)


def kernel(
    first_ref, state_hbm, weight_ref, mix_ref, out_ref,
    st, halo, patch_hi, patch_lo, weight_hl, mix_hl, inc,
    mine, pm, dr, ds, pv, ur, us, yr, ys, fs,
    local_sem, halo_send, halo_recv, pm_send, pm_recv, d_send, d_recv,
    e_send, e_recv, u_send, u_recv, y_send, y_recv, f_send, f_recv,
):
    planes16 = st.shape[0]
    channels, planes = state_hbm.shape[0], state_hbm.shape[1]
    half = st.shape[2]
    rows = 2 * half
    chunks = half // TILE
    t, g = lax.axis_index("tm"), lax.axis_index("gz")
    count = lax.axis_size("tm")
    levels = count // 4
    ring = lax.axis_size("gz")
    core = t % 2
    other = 1 - core
    side = (t // 2) % 2
    z = t // 4
    top = levels - 1
    partner = t + 1 - 2 * core
    across = t + 2 - 4 * side
    after, before = (g + 1) % ring, (g + ring - 1) % ring

    fetch = pltpu.make_async_copy(state_hbm, st.reshape(channels, planes, 2, half, 128), local_sem)
    fetch.start()

    barrier = pltpu.get_barrier_semaphore()
    pl.semaphore_signal(barrier, inc=1, device_id={"tm": partner}, device_id_type=MESH)
    pl.semaphore_signal(barrier, inc=1, device_id={"tm": across}, device_id_type=MESH)
    pl.semaphore_signal(barrier, inc=1, device_id={"gz": after}, device_id_type=MESH)
    pl.semaphore_signal(barrier, inc=1, device_id={"gz": before}, device_id_type=MESH)

    pl.semaphore_signal(barrier, inc=1, device_id={"tm": (t + 4) % count}, device_id_type=MESH)
    pl.semaphore_signal(barrier, inc=1, device_id={"tm": (t + count - 4) % count}, device_id_type=MESH)
    pl.semaphore_wait(barrier, 6)

    span = half // PIECES

    def halo_copies(piece):
        at = pl.ds(span * piece, span)
        up = pltpu.make_async_remote_copy(
            src_ref=state_hbm.at[:, planes - 1, :, at, :],
            dst_ref=halo.at[0:channels, :, at, :],
            send_sem=halo_send.at[0, piece], recv_sem=halo_recv.at[0, piece],
            device_id={"gz": after}, device_id_type=MESH,
        )
        down = pltpu.make_async_remote_copy(
            src_ref=state_hbm.at[:, 0, :, at, :],
            dst_ref=halo.at[channels : 2 * channels, :, at, :],
            send_sem=halo_send.at[1, piece], recv_sem=halo_recv.at[1, piece],
            device_id={"gz": before}, device_id_type=MESH,
        )
        return up, down

    halos = {}
    for piece in [PIECES - 1] + list(range(PIECES - 1)):
        halos[piece] = halo_copies(piece)
        for copy in halos[piece]:
            copy.start()

    fetch.wait()

    is_first = jnp.where(first_ref[0] == t, 1.0, 0.0).astype(F32)

    @pl.loop(0, planes16)
    def _(p):
        mine[p] = st[p] * is_first

    pm_copy = pltpu.make_async_remote_copy(
        src_ref=mine.at[:, other], dst_ref=pm, send_sem=pm_send, recv_sem=pm_recv,
        device_id={"tm": partner}, device_id_type=MESH,
    )
    pm_copy.start()

    high, low = split(weight_ref[...])
    wide = high.shape[0]
    weight_hl[0:wide] = high
    weight_hl[wide : 2 * wide] = low
    high, low = split(mix_ref[...])
    weight16 = high.shape[0]
    mix_hl[0:weight16] = high
    mix_hl[weight16 : 2 * weight16] = low

    st2 = st.reshape(planes16 * rows, 128)
    halo2 = halo.reshape(2 * channels * rows, 128)
    inc2 = inc.reshape(planes16 * rows, 128)
    ones = jnp.ones((8, 128), F32)

    def build(y):
        where = pl.multiple_of(BLOCK * (y + 1), 16)
        for lane, row in ((0, (y + rows) % rows), (128, (y + half) % rows)):
            body = jnp.concatenate(
                [st2[pl.ds(row, planes16, stride=rows), :], halo2[pl.ds(row, 2 * channels, stride=rows), :]], axis=0
            )
            full = jnp.concatenate([pltpu.roll(body, 1, 1), body, pltpu.roll(body, 127, 1), ones], axis=0)
            high, low = split(full)
            patch_hi[pl.ds(where, BLOCK), lane : lane + 128] = high
            patch_lo[pl.ds(where, BLOCK), lane : lane + 128] = low

    def drift(y):
        window = pl.ds(pl.multiple_of(BLOCK * y, 16), WINDOW)
        both = jnp.dot(weight_hl[...], patch_hi[window, :], preferred_element_type=F32)
        hidden = both[0:wide] + both[wide : 2 * wide] + jnp.dot(
            weight_hl[0:wide], patch_lo[window, :], preferred_element_type=F32
        )
        active = hidden + hidden * jnp.tanh(hidden)
        high, low = split(active)
        both = jnp.dot(mix_hl[...], high, preferred_element_type=F32)
        result = both[0:weight16] + both[weight16 : 2 * weight16] + jnp.dot(
            mix_hl[0:weight16], low, preferred_element_type=F32
        )
        inc2[pl.ds(y, planes16, stride=rows), :] = result[:, 0:128]
        inc2[pl.ds(y + half, planes16, stride=rows), :] = result[:, 128:256]

    def to(refs, j, part, sends, recvs, device):
        src, dst = refs
        return pltpu.make_async_remote_copy(
            src_ref=src, dst_ref=dst, send_sem=sends.at[j, part], recv_sem=recvs.at[j, part],
            device_id={"tm": device}, device_id_type=MESH,
        )

    share = planes16 // PARTS
    parts = [(part, slice(share * part, share * (part + 1))) for part in range(PARTS)]

    def at(j):
        return pl.ds(pl.multiple_of(TILE * j, TILE), TILE)

    def e_copy(j, part, w):
        return to((inc.at[w, other, at(j), :], pv.at[w, at(j), :]), j, part, e_send, e_recv, partner)

    def d_copy(j, part, w):
        return to((ds.at[w, at(j), :], dr.at[w, at(j), :]), j, part, d_send, d_recv, t - 4)

    def u_copy(j, part, w):
        return to((us.at[w, at(j), :], ur.at[w, at(j), :]), j, part, u_send, u_recv, t + 4)

    def y_copy(j, part, w):
        return to((ys.at[w, at(j), :], yr.at[w, at(j), :]), j, part, y_send, y_recv, across)

    def f_copy(j, part, w):
        return to((fs.at[w, at(j), :], out_ref.at[w, core, at(j), :]), j, part, f_send, f_recv, partner)

    pm_copy.wait()

    d_slot = 2 * (top - z)
    u_slot = 2 * z + 1 + EARLY
    y_slot = jnp.maximum(u_slot, d_slot + 1)
    f_slot = y_slot + 2
    need = {0: [PIECES - 1, 0]}
    for piece in range(1, PIECES):
        if piece < PIECES - 1:
            need[span * piece // TILE - 1] = [piece]

    def turn(n, _):
        k = n - EARLY
        for chunk, pieces in need.items():
            @pl.when(k == chunk)
            def _():
                for piece in pieces:
                    for copy in halos[piece]:
                        copy.wait_recv()

        @pl.when(k == 0)
        def _():
            build(-1)
            build(0)

        @pl.when((k >= 0) & (k < chunks))
        def _():
            first = TILE * k

            @pl.loop(0, TILE // 2)
            def _(n):
                build(first + 2 * n + 1)
                build(first + 2 * n + 2)

            @pl.loop(0, TILE // 2)
            def _(n):
                drift(first + 2 * n)
                drift(first + 2 * n + 1)

            for part, w in parts:
                e_copy(k, part, w).start()

        jd = n - d_slot

        @pl.when((jd >= 0) & (jd < chunks))
        def _():
            rows_j = at(jd)
            for part, w in parts:
                @pl.when(z < top)
                def _():
                    d_copy(jd, part, w).wait_recv()

                @pl.when(z == top)
                def _():
                    dr[w, rows_j, :] = jnp.zeros((share, TILE, 128), F32)

                @pl.when(z > 0)
                def _():
                    ds[w, rows_j, :] = dr[w, rows_j, :] + mine[w, core, rows_j, :] + pm[w, rows_j, :]
                    d_copy(jd, part, w).start()

        ju = n - u_slot

        @pl.when((ju >= 0) & (ju < chunks))
        def _():
            rows_j = at(ju)
            for part, w in parts:
                e_copy(ju, part, w).wait_recv()

                @pl.when(z > 0)
                def _():
                    u_copy(ju, part, w).wait_recv()

                @pl.when(z == 0)
                def _():
                    ur[w, rows_j, :] = jnp.zeros((share, TILE, 128), F32)

                @pl.when(z < top)
                def _():
                    us[w, rows_j, :] = (
                        ur[w, rows_j, :] + inc[w, core, rows_j, :] + pv[w, rows_j, :]
                        + mine[w, core, rows_j, :] + pm[w, rows_j, :]
                    )
                    u_copy(ju, part, w).start()

        jy = n - y_slot

        @pl.when((jy >= 0) & (jy < chunks))
        def _():
            rows_j = at(jy)
            for part, w in parts:
                total = ur[w, rows_j, :] + dr[w, rows_j, :] + mine[w, core, rows_j, :] + pm[w, rows_j, :]
                own = inc[w, core, rows_j, :] + pv[w, rows_j, :]
                ys[w, rows_j, :] = jnp.where(side == 0, total + own, total)
                y_copy(jy, part, w).start()

        jf = n - f_slot

        @pl.when((jf >= 0) & (jf < chunks))
        def _():
            rows_j = at(jf)
            for part, w in parts:
                y_copy(jf, part, w).wait_recv()
                total = (
                    ur[w, rows_j, :] + dr[w, rows_j, :] + mine[w, core, rows_j, :] + pm[w, rows_j, :]
                    + yr[w, rows_j, :]
                )
                out_ref[w, core, rows_j, :] = jnp.where(core == 1, total + pv[w, rows_j, :], total)
                fs[w, rows_j, :] = jnp.where(core == 0, total + inc[w, core, rows_j, :], total)
                f_copy(jf, part, w).start()

        return 0

    lax.fori_loop(0, chunks + 2 * top + 3 + EARLY, turn, 0)

    for pair in halos.values():
        for copy in pair:
            copy.wait_send()

    @pl.loop(0, chunks)
    def _(j):
        for part, w in parts:
            e_copy(j, part, w).wait_send()
            y_copy(j, part, w).wait_send()
            f_copy(j, part, w).wait()

            @pl.when(z > 0)
            def _():
                d_copy(j, part, w).wait_send()

            @pl.when(z < top)
            def _():
                u_copy(j, part, w).wait_send()


def shards(
    states, first_unconverged, window_offset, summaries, cond_weight, time_gain, conv_weight, out_weight
):
    channels, planes, rows, cols = states.shape[1:]
    hidden = conv_weight.shape[1]
    half = rows // 2
    steps = states.shape[0] * lax.axis_size("tm")
    step = lax.axis_index("tm")
    step_time = 1.0 - (window_offset[0] + step).astype(F32) / float(steps + 64)
    condition = jnp.dot(summaries, cond_weight, precision=lax.Precision.HIGHEST, preferred_element_type=F32)
    offset = condition + step_time * time_gain
    chosen = selector(channels, planes)
    weight = jnp.einsum("oci,oizk->zck", conv_weight, chosen, precision=lax.Precision.HIGHEST)
    marker = np.zeros((WINDOW,), np.float32)
    marker[72] = 1.0
    weight = 0.5 * (weight + offset[None, :, None] * marker).reshape(planes * hidden, WINDOW)
    mix = STEP_SIZE * jnp.einsum("ic,zw->izwc", out_weight, np.eye(planes, dtype=np.float32), precision=lax.Precision.HIGHEST)
    mix = mix.reshape(channels * planes, planes * hidden)
    state = states.reshape(channels, planes, 2, half, cols)
    p16 = channels * planes
    chunks = half // TILE
    half_shape = pltpu.VMEM((p16, half, cols), F32)
    whole_shape = pltpu.VMEM((p16, 2, half, cols), F32)
    dma = pltpu.SemaphoreType.DMA
    out = pl.pallas_call(
        kernel,
        name="picard",
        out_shape=jax.ShapeDtypeStruct((p16, 2, half, cols), F32),
        in_specs=[
            pl.BlockSpec(memory_space=pltpu.SMEM),
            pl.BlockSpec(memory_space=pl.ANY),
            pl.BlockSpec(memory_space=pltpu.VMEM),
            pl.BlockSpec(memory_space=pltpu.VMEM),
        ],
        out_specs=pl.BlockSpec(memory_space=pltpu.VMEM),
        scratch_shapes=[
            whole_shape,
            pltpu.VMEM((2 * channels, 2, half, cols), F32),
            pltpu.VMEM(((half + 2) * BLOCK, 256), BF16),
            pltpu.VMEM(((half + 2) * BLOCK, 256), BF16),
            pltpu.VMEM((2 * planes * hidden, WINDOW), BF16),
            pltpu.VMEM((2 * p16, planes * hidden), BF16),
            whole_shape,
            whole_shape,
        ]
        + [half_shape] * 9
        + [dma, dma((2, PIECES)), dma((2, PIECES)), dma, dma]
        + [dma((chunks, PARTS))] * 10,
        compiler_params=pltpu.CompilerParams(
            collective_id=0, has_side_effects=True, vmem_limit_bytes=48 * 1024 * 1024
        ),
    )(first_unconverged, state, weight, mix)
    return out.reshape(states.shape)


def solution(mesh):
    placed = (P("tm", None, "gz", None, None), P(), P(), P(), P(), P(), P(), P())
    return jax.shard_map(
        shards,
        mesh=mesh,
        in_specs=placed,
        out_specs=P("tm", None, "gz", None, None),
        check_vma=False,
    )
```

```python
import functools

import jax
import jax.numpy as jnp
import numpy as np
from jax import lax
from jax.experimental import pallas as pl
from jax.experimental.pallas import tpu as pltpu
from jax.sharding import PartitionSpec as P

STEP_SIZE = 0.125
MESH = pl.DeviceIdType.MESH

BLOCK = 80
WINDOW = 3 * BLOCK
TILE = 8
PIECES = 8
EARLY = 4
PARTS = 2
F32, BF16 = jnp.float32, jnp.bfloat16


def selector(channels, planes):
    chosen = np.zeros((27, channels, planes, WINDOW), np.float32)
    for b in range(3):
        for e in range(3):
            for zo in range(planes):
                for a in range(3):
                    zi = zo + a - 1
                    for i in range(channels):
                        if zi < 0:
                            plane = channels * planes + i
                        elif zi >= planes:
                            plane = channels * planes + channels + i
                        else:
                            plane = i * planes + zi
                        chosen[9 * a + 3 * b + e, i, zo, BLOCK * b + 24 * e + plane] = 1.0
    return chosen


def split(value):
    high = value.astype(BF16)
    return high, (value - high.astype(F32)).astype(BF16)


def kernel(
    first_ref, state_hbm, weight_ref, mix_ref, out_ref,
    st, halo, patch_hi, patch_lo, weight_hl, mix_hl, inc,
    mine, pm, dr, ds, pv, ur, us, yr, ys, fs,
    local_sem, halo_send, halo_recv, pm_send, pm_recv, d_send, d_recv,
    e_send, e_recv, u_send, u_recv, y_send, y_recv, f_send, f_recv,
):
    planes16 = st.shape[0]
    channels, planes = state_hbm.shape[0], state_hbm.shape[1]
    half = st.shape[2]
    rows = 2 * half
    chunks = half // TILE
    t, g = lax.axis_index("tm"), lax.axis_index("gz")
    count = lax.axis_size("tm")
    levels = count // 4
    ring = lax.axis_size("gz")
    core = t % 2
    other = 1 - core
    side = (t // 2) % 2
    z = t // 4
    top = levels - 1
    partner = t + 1 - 2 * core
    across = t + 2 - 4 * side
    after, before = (g + 1) % ring, (g + ring - 1) % ring

    fetch = pltpu.make_async_copy(state_hbm, st.reshape(channels, planes, 2, half, 128), local_sem)
    fetch.start()

    barrier = pltpu.get_barrier_semaphore()
    pl.semaphore_signal(barrier, inc=1, device_id={"tm": partner}, device_id_type=MESH)
    pl.semaphore_signal(barrier, inc=1, device_id={"tm": across}, device_id_type=MESH)
    pl.semaphore_signal(barrier, inc=1, device_id={"gz": after}, device_id_type=MESH)
    pl.semaphore_signal(barrier, inc=1, device_id={"gz": before}, device_id_type=MESH)

    pl.semaphore_signal(barrier, inc=1, device_id={"tm": (t + 4) % count}, device_id_type=MESH)
    pl.semaphore_signal(barrier, inc=1, device_id={"tm": (t + count - 4) % count}, device_id_type=MESH)
    pl.semaphore_wait(barrier, 6)

    span = half // PIECES

    def halo_copies(piece):
        at = pl.ds(span * piece, span)
        up = pltpu.make_async_remote_copy(
            src_ref=state_hbm.at[:, planes - 1, :, at, :],
            dst_ref=halo.at[0:channels, :, at, :],
            send_sem=halo_send.at[0, piece], recv_sem=halo_recv.at[0, piece],
            device_id={"gz": after}, device_id_type=MESH,
        )
        down = pltpu.make_async_remote_copy(
            src_ref=state_hbm.at[:, 0, :, at, :],
            dst_ref=halo.at[channels : 2 * channels, :, at, :],
            send_sem=halo_send.at[1, piece], recv_sem=halo_recv.at[1, piece],
            device_id={"gz": before}, device_id_type=MESH,
        )
        return up, down

    halos = {}
    for piece in [PIECES - 1] + list(range(PIECES - 1)):
        halos[piece] = halo_copies(piece)
        for copy in halos[piece]:
            copy.start()

    fetch.wait()

    is_first = jnp.where(first_ref[0] == t, 1.0, 0.0).astype(F32)

    @pl.loop(0, planes16)
    def _(p):
        mine[p] = st[p] * is_first

    pm_copy = pltpu.make_async_remote_copy(
        src_ref=mine.at[:, other], dst_ref=pm, send_sem=pm_send, recv_sem=pm_recv,
        device_id={"tm": partner}, device_id_type=MESH,
    )
    pm_copy.start()

    high, low = split(weight_ref[...])
    wide = high.shape[0]
    weight_hl[0:wide] = high
    weight_hl[wide : 2 * wide] = low
    high, low = split(mix_ref[...])
    weight16 = high.shape[0]
    mix_hl[0:weight16] = high
    mix_hl[weight16 : 2 * weight16] = low

    st2 = st.reshape(planes16 * rows, 128)
    halo2 = halo.reshape(2 * channels * rows, 128)
    inc2 = inc.reshape(planes16 * rows, 128)
    ones = jnp.ones((8, 128), F32)

    def build(y):
        where = pl.multiple_of(BLOCK * (y + 1), 16)
        for lane, row in ((0, (y + rows) % rows), (128, (y + half) % rows)):
            body = jnp.concatenate(
                [st2[pl.ds(row, planes16, stride=rows), :], halo2[pl.ds(row, 2 * channels, stride=rows), :]], axis=0
            )
            full = jnp.concatenate([pltpu.roll(body, 1, 1), body, pltpu.roll(body, 127, 1), ones], axis=0)
            high, low = split(full)
            patch_hi[pl.ds(where, BLOCK), lane : lane + 128] = high
            patch_lo[pl.ds(where, BLOCK), lane : lane + 128] = low

    def drift(y):
        window = pl.ds(pl.multiple_of(BLOCK * y, 16), WINDOW)
        both = jnp.dot(weight_hl[...], patch_hi[window, :], preferred_element_type=F32)
        hidden = both[0:wide] + both[wide : 2 * wide] + jnp.dot(
            weight_hl[0:wide], patch_lo[window, :], preferred_element_type=F32
        )
        active = hidden + hidden * jnp.tanh(hidden)
        high, low = split(active)
        both = jnp.dot(mix_hl[...], high, preferred_element_type=F32)
        result = both[0:weight16] + both[weight16 : 2 * weight16] + jnp.dot(
            mix_hl[0:weight16], low, preferred_element_type=F32
        )
        inc2[pl.ds(y, planes16, stride=rows), :] = result[:, 0:128]
        inc2[pl.ds(y + half, planes16, stride=rows), :] = result[:, 128:256]

    def to(refs, j, part, sends, recvs, device):
        src, dst = refs
        return pltpu.make_async_remote_copy(
            src_ref=src, dst_ref=dst, send_sem=sends.at[j, part], recv_sem=recvs.at[j, part],
            device_id={"tm": device}, device_id_type=MESH,
        )

    share = planes16 // PARTS
    parts = [(part, slice(share * part, share * (part + 1))) for part in range(PARTS)]

    def at(j):
        return pl.ds(pl.multiple_of(TILE * j, TILE), TILE)

    def e_copy(j, part, w):
        return to((inc.at[w, other, at(j), :], pv.at[w, at(j), :]), j, part, e_send, e_recv, partner)

    def d_copy(j, part, w):
        return to((ds.at[w, at(j), :], dr.at[w, at(j), :]), j, part, d_send, d_recv, t - 4)

    def u_copy(j, part, w):
        return to((us.at[w, at(j), :], ur.at[w, at(j), :]), j, part, u_send, u_recv, t + 4)

    def y_copy(j, part, w):
        return to((ys.at[w, at(j), :], yr.at[w, at(j), :]), j, part, y_send, y_recv, across)

    def f_copy(j, part, w):
        return to((fs.at[w, at(j), :], out_ref.at[w, core, at(j), :]), j, part, f_send, f_recv, partner)

    pm_copy.wait()

    d_slot = 2 * (top - z)
    u_slot = 2 * z + 1 + EARLY
    y_slot = jnp.maximum(u_slot, d_slot + 1)
    f_slot = y_slot + 2
    need = {0: [PIECES - 1, 0]}
    for piece in range(1, PIECES):
        if piece < PIECES - 1:
            need.setdefault(span * piece // TILE - 1, []).append(piece)

    def turn(n, _):
        k = n - EARLY
        for chunk, pieces in need.items():
            @pl.when(k == chunk)
            def _():
                for piece in pieces:
                    for copy in halos[piece]:
                        copy.wait_recv()

        @pl.when(k == 0)
        def _():
            for y in range(-1, 3):
                build(y)

        @pl.when((k >= 0) & (k < chunks))
        def _():
            first = TILE * k

            @pl.loop(0, TILE // 2)
            def _(n):
                drift(first + 2 * n)
                drift(first + 2 * n + 1)
                build(first + 2 * n + 3)
                build(first + 2 * n + 4)

            for part, w in parts:
                e_copy(k, part, w).start()

        jd = n - d_slot

        @pl.when((jd >= 0) & (jd < chunks))
        def _():
            rows_j = at(jd)
            for part, w in parts:
                @pl.when(z < top)
                def _():
                    d_copy(jd, part, w).wait_recv()

                @pl.when(z == top)
                def _():
                    dr[w, rows_j, :] = jnp.zeros((share, TILE, 128), F32)

                @pl.when(z > 0)
                def _():
                    ds[w, rows_j, :] = dr[w, rows_j, :] + mine[w, core, rows_j, :] + pm[w, rows_j, :]
                    d_copy(jd, part, w).start()

        ju = n - u_slot

        @pl.when((ju >= 0) & (ju < chunks))
        def _():
            rows_j = at(ju)
            for part, w in parts:
                e_copy(ju, part, w).wait_recv()

                @pl.when(z > 0)
                def _():
                    u_copy(ju, part, w).wait_recv()

                @pl.when(z == 0)
                def _():
                    ur[w, rows_j, :] = jnp.zeros((share, TILE, 128), F32)

                @pl.when(z < top)
                def _():
                    us[w, rows_j, :] = (
                        ur[w, rows_j, :] + inc[w, core, rows_j, :] + pv[w, rows_j, :]
                        + mine[w, core, rows_j, :] + pm[w, rows_j, :]
                    )
                    u_copy(ju, part, w).start()

        jy = n - y_slot

        @pl.when((jy >= 0) & (jy < chunks))
        def _():
            rows_j = at(jy)
            for part, w in parts:
                total = ur[w, rows_j, :] + dr[w, rows_j, :] + mine[w, core, rows_j, :] + pm[w, rows_j, :]
                own = inc[w, core, rows_j, :] + pv[w, rows_j, :]
                ys[w, rows_j, :] = jnp.where(side == 0, total + own, total)
                y_copy(jy, part, w).start()

        jf = n - f_slot

        @pl.when((jf >= 0) & (jf < chunks))
        def _():
            rows_j = at(jf)
            for part, w in parts:
                y_copy(jf, part, w).wait_recv()
                total = (
                    ur[w, rows_j, :] + dr[w, rows_j, :] + mine[w, core, rows_j, :] + pm[w, rows_j, :]
                    + yr[w, rows_j, :]
                )
                out_ref[w, core, rows_j, :] = jnp.where(core == 1, total + pv[w, rows_j, :], total)
                fs[w, rows_j, :] = jnp.where(core == 0, total + inc[w, core, rows_j, :], total)
                f_copy(jf, part, w).start()

        return 0

    lax.fori_loop(0, chunks + 2 * top + 3 + EARLY, turn, 0)

    for pair in halos.values():
        for copy in pair:
            copy.wait_send()

    @pl.loop(0, chunks)
    def _(j):
        for part, w in parts:
            e_copy(j, part, w).wait_send()
            y_copy(j, part, w).wait_send()
            f_copy(j, part, w).wait()

            @pl.when(z > 0)
            def _():
                d_copy(j, part, w).wait_send()

            @pl.when(z < top)
            def _():
                u_copy(j, part, w).wait_send()


def shards(
    states, first_unconverged, window_offset, summaries, cond_weight, time_gain, conv_weight, out_weight
):
    channels, planes, rows, cols = states.shape[1:]
    hidden = conv_weight.shape[1]
    half = rows // 2
    steps = states.shape[0] * lax.axis_size("tm")
    step = lax.axis_index("tm")
    step_time = 1.0 - (window_offset[0] + step).astype(F32) / float(steps + 64)
    condition = jnp.dot(summaries, cond_weight, precision=lax.Precision.HIGHEST, preferred_element_type=F32)
    offset = condition + step_time * time_gain
    chosen = selector(channels, planes)
    weight = jnp.einsum("oci,oizk->zck", conv_weight, chosen, precision=lax.Precision.HIGHEST)
    marker = np.zeros((WINDOW,), np.float32)
    marker[72] = 1.0
    weight = 0.5 * (weight + offset[None, :, None] * marker).reshape(planes * hidden, WINDOW)
    mix = STEP_SIZE * jnp.einsum("ic,zw->izwc", out_weight, np.eye(planes, dtype=np.float32), precision=lax.Precision.HIGHEST)
    mix = mix.reshape(channels * planes, planes * hidden)
    state = states.reshape(channels, planes, 2, half, cols)
    p16 = channels * planes
    chunks = half // TILE
    half_shape = pltpu.VMEM((p16, half, cols), F32)
    whole_shape = pltpu.VMEM((p16, 2, half, cols), F32)
    dma = pltpu.SemaphoreType.DMA
    out = pl.pallas_call(
        kernel,
        name="picard",
        out_shape=jax.ShapeDtypeStruct((p16, 2, half, cols), F32),
        in_specs=[
            pl.BlockSpec(memory_space=pltpu.SMEM),
            pl.BlockSpec(memory_space=pl.ANY),
            pl.BlockSpec(memory_space=pltpu.VMEM),
            pl.BlockSpec(memory_space=pltpu.VMEM),
        ],
        out_specs=pl.BlockSpec(memory_space=pltpu.VMEM),
        scratch_shapes=[
            whole_shape,
            pltpu.VMEM((2 * channels, 2, half, cols), F32),
            pltpu.VMEM(((half + 4) * BLOCK, 256), BF16),
            pltpu.VMEM(((half + 4) * BLOCK, 256), BF16),
            pltpu.VMEM((2 * planes * hidden, WINDOW), BF16),
            pltpu.VMEM((2 * p16, planes * hidden), BF16),
            whole_shape,
            whole_shape,
        ]
        + [half_shape] * 9
        + [dma, dma((2, PIECES)), dma((2, PIECES)), dma, dma]
        + [dma((chunks, PARTS))] * 10,
        compiler_params=pltpu.CompilerParams(
            collective_id=0, has_side_effects=True, vmem_limit_bytes=48 * 1024 * 1024
        ),
    )(first_unconverged, state, weight, mix)
    return out.reshape(states.shape)


def solution(mesh):
    placed = (P("tm", None, "gz", None, None), P(), P(), P(), P(), P(), P(), P())
    return jax.shard_map(
        shards,
        mesh=mesh,
        in_specs=placed,
        out_specs=P("tm", None, "gz", None, None),
        check_vma=False,
    )
```
